32 devices in a mesh: blk: 8 (over z, x), rep: 4 (over y, core).
Axes of the slice: x: 2, y: 2, z: 4, core: 2. Of those that a mesh axis runs over, the one named last changes fastest.
Arguments:
- features: bfloat16 [4096, 256], P(('blk', 'rep')), may hold values from -6 to 6
- adjacency_tiles: bfloat16 [512, 128, 128], P(('blk', 'rep')), may hold values from -0.125 to 0.125
- tile_rows: int32 [512], P(('blk', 'rep')), may hold values from 0 to 4, as said below
- weight: bfloat16 [256, 256], P('rep'), may hold values from -0.375 to 0.375
- cotangent: bfloat16 [4096, 256], P(('blk', 'rep')), may hold values from -6 to 6
Outputs:
- activations: bfloat16 [4096, 256], P(('blk', 'rep'))
- grad_weight: float32 [256, 256], P('rep')
- grad_features: float32 [4096, 256], P(('blk', 'rep'))
The draws below stay inside these ranges and needn't reach their ends.
Inputs may be any that keep to these rules, and one draw needn't show every extreme that they name: `tile_rows`: within each device's slots, the 2 slots of one column block name different row blocks or are empty; the first slot of every column block is never empty.
All inputs are finite; a program needn't handle non-finite values.
Results may differ from the reference program's by a relative error of at most 0.014.
Values may be sent and summed in bfloat16 or wider, within the bound.
No kernel may reach another device: no remote copies, remote signals or barrier semaphores. Data moves between devices by JAX's collectives and lax.ppermute only.
A program may use at most 64 MiB of HBM per device.

```python
import math
import jax
import jax.numpy as jnp
from jax import lax

F = 256
BS = 128
SLOTS = 2
BR = 1
RB = 4
TSLOTS = 16
NODES = 4096
N_BLK = 8
N_REP = 4


def draw_tile_rows(key, part):
    groups = N_BLK * N_REP * TSLOTS // SLOTS
    keys = jax.random.split(jax.random.fold_in(key, 11), groups)
    choices_rows = jax.vmap(lambda single: jax.random.permutation(single, RB)[:SLOTS])(keys)
    level = jax.random.randint(jax.random.fold_in(key, 12), (N_BLK * N_REP, 1), 0, 4)
    level = jnp.repeat(level, TSLOTS // SLOTS, axis=0)
    coins = jax.random.randint(jax.random.fold_in(key, 13), (groups, SLOTS), 0, 4)
    first_slot = jnp.arange(SLOTS, dtype=jnp.int32)[None, :] == 0
    keep = (coins < level) | first_slot
    rows_all = jnp.where(keep, choices_rows, RB)
    rows_all = rows_all.at[0, SLOTS - 1].set(RB)
    return rows_all.reshape(-1).astype(jnp.int32)


def block_scale(rng, shape, cuts, least, largest):
    def one(dim, parts):
        draws = jax.random.uniform(jax.random.fold_in(jax.random.fold_in(rng, 6), dim), (parts,), jnp.float32, least / len(cuts), largest / len(cuts))
        return jnp.repeat(jnp.exp(draws), shape[dim] // parts).reshape((-1,) + (1,) * (len(shape) - dim - 1))

    level = one(*cuts[0])
    for cut in cuts[1:]:
        level = level * one(*cut)
    return level


def normal_values(rng, extent, width, limit, pieces=(), kind=jnp.bfloat16):
    result = jax.random.normal(rng, extent, jnp.float32) * width
    if len(pieces) > 0:
        result = block_scale(rng, extent, pieces, -0.22, 0.18) * result
    return jnp.clip(result, min=-limit, max=limit).astype(kind)


def setup_inputs(seed: int = 0) -> dict:
    key_of = jax.random.split(jax.random.key(seed), 6)
    return {
        "features": normal_values(key_of[0], (NODES, F), 1.0, 6.0, ((0, 32),)),
        "adjacency_tiles": normal_values(key_of[1], (N_BLK * N_REP * TSLOTS, BS, BS), (N_BLK * SLOTS * BS) ** -0.5, 0.125, ((0, 32),)),
        "tile_rows": draw_tile_rows(jax.random.fold_in(key_of[5], 71), 0),
        "weight": normal_values(key_of[3], (F, F), F ** -0.5, 0.375, ((0, 4),)),
        "cotangent": normal_values(key_of[4], (NODES, F), 1.0, 6.0, ((0, 32),)),
    }


def reference(features, adjacency_tiles, tile_rows, weight, cotangent):
    panels = features.reshape(NODES // BS, BS, F).astype(jnp.float32)
    tiles_dev = adjacency_tiles.reshape(N_BLK * N_REP, TSLOTS, BS, BS)
    rows_dev = tile_rows.reshape(N_BLK * N_REP, TSLOTS)
    devices = jnp.arange(N_BLK * N_REP, dtype=jnp.int32)
    slot_index = jnp.arange(TSLOTS, dtype=jnp.int32)
    column_group = slot_index // SLOTS
    source = column_group // BR
    sub_block = column_group % BR
    row_ids = jnp.arange(RB, dtype=jnp.int32)

    def columns_of(device):
        return ((source * N_REP + device % N_REP) * BR + sub_block).astype(jnp.int32)

    def forward_step(total, items):
        tiles_one, rows_one, device = items
        cols = columns_of(device)
        picked = (rows_one[:, None] == row_ids[None, :]).astype(jnp.float32)
        gathered = panels[cols]
        products = jnp.einsum('tij,tjf->tif', tiles_one.astype(jnp.float32), gathered, precision=lax.Precision.HIGHEST)
        added = jnp.einsum('tr,tif->rif', picked, products, precision=lax.Precision.HIGHEST)
        first = (device // N_REP * RB).astype(jnp.int32)
        current = lax.dynamic_slice_in_dim(total, first, RB, 0)
        return (lax.dynamic_update_slice_in_dim(total, current + added, first, 0), None)
    start_total = jnp.zeros((NODES // BS, BS, F), jnp.float32)
    total, _ = lax.scan(forward_step, start_total, (tiles_dev, rows_dev, devices))
    aggregated = total.reshape(NODES, F).astype(jnp.bfloat16)
    pre = jnp.dot(aggregated, weight, preferred_element_type=jnp.float32)
    gate_sig = jax.nn.sigmoid(pre)
    activations = (pre * gate_sig).astype(jnp.bfloat16)
    dpre = (cotangent.astype(jnp.float32) * gate_sig * (1.0 + pre * (1.0 - gate_sig))).astype(jnp.bfloat16)
    grad_weight = jnp.dot(aggregated.T, dpre, preferred_element_type=jnp.float32) * (1.0 / math.sqrt(NODES))
    dagg = jnp.dot(dpre, weight.T, preferred_element_type=jnp.float32).astype(jnp.bfloat16)
    dagg_panels = dagg.reshape(NODES // BS, BS, F).astype(jnp.float32)

    def backward_step(total, items):
        tiles_one, rows_one, device = items
        cols = columns_of(device)
        picked = (rows_one[:, None] == row_ids[None, :]).astype(jnp.float32)
        first = (device // N_REP * RB).astype(jnp.int32)
        group_rows = lax.dynamic_slice_in_dim(dagg_panels, first, RB, 0)
        selected = jnp.einsum('tr,rif->tif', picked, group_rows, precision=lax.Precision.HIGHEST)
        terms = jnp.einsum('tij,tif->tjf', tiles_one.astype(jnp.float32), selected, precision=lax.Precision.HIGHEST)
        return (total.at[cols].add(terms), None)
    grad_total, _ = lax.scan(backward_step, jnp.zeros((NODES // BS, BS, F), jnp.float32), (tiles_dev, rows_dev, devices))
    grad_features = grad_total.reshape(NODES, F)
    return (activations, grad_weight, grad_features)
```

```python
import functools
import math

import jax
import jax.numpy as jnp
from jax import lax
from jax.experimental import pallas as pl
from jax.experimental.pallas import tpu as pltpu
from jax.sharding import PartitionSpec as P

SLOTS = 2
CORES = 2
MOST = 4


bf16 = jnp.bfloat16
f32 = jnp.float32
VMEM = pl.BlockSpec(memory_space=pltpu.VMEM)
SMEM = pl.BlockSpec(memory_space=pltpu.SMEM)


def struct(shape, dtype):
    return pltpu.VMEM(shape, dtype)


def final(shape, dtype):
    return jax.ShapeDtypeStruct(shape, dtype)


def call(body, name, outs, ins, in_specs=None, scratch=(), room=None):
    in_specs = in_specs or [VMEM] * len(ins)
    ins = [
        pltpu.with_memory_space_constraint(x, pltpu.VMEM) if spec is VMEM else x
        for x, spec in zip(ins, in_specs)
    ]
    if room is None:
        held = [*outs, *outs, *scratch, *scratch, *ins[1:]]
        room = sum(math.prod(x.shape) * jnp.dtype(x.dtype).itemsize for x in held)
    return pl.pallas_call(
        body,
        name=name,
        out_shape=tuple(outs),
        in_specs=in_specs,
        out_specs=tuple(VMEM for _ in outs),
        scratch_shapes=list(scratch),
        compiler_params=pltpu.CompilerParams(vmem_limit_bytes=room + (2 << 20)),
    )(*ins)


def stages_of(count):
    assert count & (count - 1) == 0
    stages, stride = [], 1
    while stride < count:
        size = 2 if (count // stride).bit_length() % 2 == 0 else 4
        stages.append((stride, size))
        stride *= size
    return stages


def send(value, axis, bits):
    count = lax.axis_size(axis)
    return lax.ppermute(value, axis, [(i, i ^ bits) for i in range(count)])


def dot(a, b):
    return jnp.dot(a, b, preferred_element_type=f32)


def panel_kernel(order, group, half, size, rows, tiles, fwd, bwd):
    blk, core = lax.axis_index("blk"), lax.axis_index("rep") % CORES
    fwd[...] = jnp.zeros_like(fwd)
    bwd[...] = jnp.zeros_like(bwd)
    for q, p in enumerate(order):
        for k in range(SLOTS):
            t = (blk ^ p) * SLOTS + k
            g = rows[t]
            pos = jnp.where(g < group, ((g % CORES) ^ core) * half + g // CORES, group)
            tile = tiles[t]
            fwd[pos, :, q * size : (q + 1) * size] = tile
            bwd[pos, q * size : (q + 1) * size, :] = tile.T


def weight_kernel(*refs):
    *parts, full = refs
    rows = parts[0].shape[0]
    for j, part in enumerate(parts):
        full[lax.axis_index("rep") ^ j] = part[...]


def early_kernel(cols, size, group, panel, *refs):
    *blocks, out = refs
    rows = group * size
    out[...] = dot(
        panel[:group, :, : len(blocks) * size].reshape(rows, len(blocks) * size),
        jnp.concatenate([x[...] for x in blocks], axis=0),
    )


def late_kernel(first, size, group, half, panel, early, *refs):
    *blocks, own, away = refs
    cols = slice(first * size, (first + len(blocks)) * size)
    x = jnp.concatenate([v[...] for v in blocks], axis=0)
    width = len(blocks) * size
    cut = half * size
    away[...] = (
        early[cut:] + dot(panel[half:group, :, cols].reshape(cut, width), x)
    ).astype(bf16)
    own[...] = early[:cut] + dot(panel[:half, :, cols].reshape(cut, width), x)


def pair_kernel(own, came, total, away):
    value = own[...] + came[...].astype(f32)
    total[...] = value
    away[...] = value.astype(bf16)


def dense_kernel(half, size, total, weight, *refs):
    came = refs[: half - 1]
    cots = refs[half - 1 : 2 * half - 1]
    acts, dagg, msg, wown, agg_s, pre_s, dpre_s, wg_s = refs[2 * half - 1 :]
    rep = lax.axis_index("rep")
    y, core = rep // CORES, rep % CORES
    rows = half * size
    feat = total.shape[1]
    agg = total[...]
    for v in came:
        agg = agg + v[...].astype(f32)
    agg = agg.astype(bf16)
    agg_s[...] = agg
    w = weight[...].reshape(feat, feat)
    pre_s[...] = dot(agg, w).reshape(half, size, feat)
    for j, cot in enumerate(cots):
        pre = pre_s[y ^ j]
        gate = jax.nn.sigmoid(pre)
        if j == 0:
            acts[...] = (pre * gate).astype(bf16)
        dpre_s[y ^ j] = (
            cot[...].astype(f32) * gate * (1.0 + pre * (1.0 - gate))
        ).astype(bf16)
    dpre = dpre_s[...].reshape(rows, feat)
    back = lax.dot_general(
        dpre, w, (((1,), (1,)), ((), ())), preferred_element_type=f32
    ).astype(bf16)
    dagg[...] = back
    msg[:rows] = back
    part = feat // half
    cols = agg_s[:, pl.ds(pl.multiple_of(y * part, part), part)]
    wg_s[...] = lax.dot_general(
        cols, dpre, (((0,), (0,)), ((), ())), preferred_element_type=f32
    ).reshape(wg_s.shape)
    wown[...] = wg_s[core]
    msg[rows:] = wg_s[1 - core].astype(bf16)


def terms_of(panel, dagg, msg, half, size, first, last):
    rows = half * size
    cut = slice(first * size, last * size)
    out = None
    for i in range(half):
        mine = dot(panel[i, cut], dagg[i * size : (i + 1) * size])
        theirs = dot(panel[half + i, cut], msg[i * size : (i + 1) * size])
        out = mine + theirs if out is None else out + mine + theirs
    return out


def away_kernel(half, size, keep, panel, dagg, msg, wown, *refs):
    *outs, wsum = refs
    rows = half * size
    total = wown[...] + msg[rows:].astype(f32)
    wsum[...] = total
    for j, out in enumerate(outs):
        first = (j + 1) * keep
        out[: keep * size] = terms_of(panel, dagg, msg, half, size, first, first + keep).astype(bf16)
        out[keep * size :] = total.astype(bf16)


def keep_kernel(half, size, keep, panel, dagg, msg, out):
    out[...] = terms_of(panel, dagg, msg, half, size, 0, keep)


def fold_kernel(rows, kept, wsum, *refs):
    came, outs, gone, wgone = refs
    value, wvalue = kept[...], wsum[...]
    for v in came:
        value = value + v[: kept.shape[0]].astype(f32)
        wvalue = wvalue + v[kept.shape[0] :].astype(f32)
    gone[...] = value[:rows]
    wgone[...] = wvalue
    for j, out in enumerate(outs):
        out[:rows] = value[(j + 1) * rows : (j + 2) * rows].astype(bf16)
        out[rows:] = wvalue.astype(bf16)


def last_kernel(scale, kept, wsum, *refs):
    *came, grad, wgrad = refs
    rows = kept.shape[0]
    value, wvalue = kept[...], wsum[...]
    for v in came:
        value = value + v[:rows].astype(f32)
        wvalue = wvalue + v[rows:].astype(f32)
    grad[...] = value
    wgrad[...] = wvalue * scale


def shards(features, adjacency_tiles, tile_rows, weight, cotangent):
    blocks, reps = lax.axis_size("blk"), lax.axis_size("rep")
    size, feat = features.shape
    group = reps
    half = reps // CORES
    assert size == adjacency_tiles.shape[1] and reps % CORES == 0
    stages = stages_of(blocks)

    def digits(p):
        return tuple((p // stride) % count for stride, count in stages)

    order = sorted(range(blocks), key=digits)
    held = {0: features}
    for stride, count in reversed(stages):
        for j in reversed(range(1, count)):
            ready = [p for p in held if p % (stride * count) // stride == 0]
            if len(ready) > MOST:
                moved = send(jnp.concatenate([held[p] for p in ready]), "blk", j * stride)
                moved = jnp.split(moved, len(ready))
            else:
                moved = [send(held[p], "blk", j * stride) for p in ready]
            held.update((p | j * stride, v) for p, v in zip(ready, moved))
    weights = [weight] + [send(weight, "rep", j) for j in range(1, reps)]
    cots = [cotangent] + [send(cotangent, "rep", j * CORES) for j in range(1, half)]

    fwd, bwd = call(
        functools.partial(panel_kernel, order, group, half, size),
        "panels",
        [struct((group + 1, size, blocks * size), bf16), struct((group + 1, blocks * size, size), bf16)],
        (tile_rows, adjacency_tiles),
        [SMEM, VMEM],
        room=0,
    )
    (full,) = call(
        weight_kernel,
        "weights",
        [struct((reps,) + weight.shape, bf16)],
        weights,
    )
    keep = blocks // stages[0][1]
    (early,) = call(
        functools.partial(early_kernel, None, size, group),
        "early",
        [struct((group * size, feat), f32)],
        (fwd, *[held[p] for p in order[:keep]]),
    )
    rows = half * size
    own, away = call(
        functools.partial(late_kernel, keep, size, group, half),
        "late",
        [struct((rows, feat), f32), struct((rows, feat), bf16)],
        (fwd, early, *[held[p] for p in order[keep:]]),
    )
    total, away = call(
        pair_kernel, "pair", [struct((rows, feat), f32), struct((rows, feat), bf16)], (own, send(away, "rep", 1))
    )
    came = [send(away, "rep", j * CORES) for j in range(1, half)]
    wrows = weight.shape[0]
    acts, dagg, msg, wown = call(
        functools.partial(dense_kernel, half, size),
        "dense",
        [
            final((size, feat), bf16),
            struct((rows, feat), bf16),
            struct((rows + wrows, feat), bf16),
            struct((wrows, feat), f32),
        ],
        (total, full, *came, *cots),
        None,
        [
            pltpu.VMEM((rows, feat), bf16),
            pltpu.VMEM((half, size, feat), f32),
            pltpu.VMEM((half, size, feat), bf16),
            pltpu.VMEM((CORES, wrows, feat), f32),
        ],
    )
    msg = send(msg, "rep", 1)
    outs = call(
        functools.partial(away_kernel, half, size, keep),
        "away",
        [struct((keep * size + wrows, feat), bf16)] * (stages[0][1] - 1) + [struct((wrows, feat), f32)],
        (bwd, dagg, msg, wown),
    )
    *aways, wsum = outs
    (kept,) = call(
        functools.partial(keep_kernel, half, size, keep), "keep", [struct((keep * size, feat), f32)], (bwd, dagg, msg)
    )
    for i, (stride, count) in enumerate(stages):
        came = [send(v, "blk", (j + 1) * stride) for j, v in enumerate(aways)]
        if i + 1 == len(stages):
            break
        nexts = stages[i + 1][1]
        nrows = kept.shape[0] // nexts

        def fold(kept_ref, wsum_ref, *refs, n=len(came), rows=nrows):
            fold_kernel(rows, kept_ref, wsum_ref, refs[:n], refs[n + 2 :], refs[n], refs[n + 1])

        kept, wsum, *aways = call(
            fold,
            f"fold{i}",
            [struct((nrows, feat), f32), struct((wrows, feat), f32)]
            + [struct((nrows + wrows, feat), bf16)] * (nexts - 1),
            (kept, wsum, *came),
        )
    grad, wgrad = call(
        functools.partial(last_kernel, 1.0 / math.sqrt(blocks * reps * size)),
        "last",
        [final((size, feat), f32), final((wrows, feat), f32)],
        (kept, wsum, *came),
    )
    return acts, wgrad, grad


def solution(mesh):
    both = P(("blk", "rep"), None)
    return jax.shard_map(
        shards,
        mesh=mesh,
        in_specs=(both, P(("blk", "rep"), None, None), P(("blk", "rep")), P("rep", None), both),
        out_specs=(both, P("rep", None), both),
        check_vma=False,
    )
```
